32 devices in a mesh: gx: 8 (over z, x), gy: 4 (over y, core).
Axes of the slice: x: 2, y: 2, z: 4, core: 2. Of those that a mesh axis runs over, the one named last changes fastest.
Arguments:
- positions: float32 [3, 65536], P(None, ('gx', 'gy')), may hold values from -6 to 6
- velocities: float32 [3, 65536], P(None, ('gx', 'gy')), may hold values from -6 to 6
- masses: float32 [65536], P(('gx', 'gy')), may hold values from 0.25 to 4
- labels: int32 [65536, 1], P(('gx', 'gy')), may hold values from 0 to 255; in each aligned block of 2048 rows (0 to 2047, 2048 to 4095, ...) at most 16 rows name the same one
- owner_slot: int32 [256], replicated, may hold values from 0 to 255, each once
- group_cap: int32 [256], replicated, may hold values from 512 to 4095
Outputs:
- compact_index: int32 [65536], P(('gx', 'gy'))
- potential: float32 [65536], P(('gx', 'gy'))
- binding: float32 [65536], P(('gx', 'gy'))
- catalog: float32 [4, 256], P(None, ('gx', 'gy'))
The draws below stay inside these ranges and needn't reach their ends.
Inputs may be any that keep to these rules, and one draw needn't show every extreme that they name: `labels`: on each device's 2048 particles no label occurs more than 16 times; some label occurs exactly 16 times in some devices' particles; every label occurs somewhere. `owner_slot` is a permutation. Group g is owned by device owner_slot[g] // 8 (devices numbered along gx then gy) as its local group owner_slot[g] % 8.
All inputs are finite; a program needn't handle non-finite values.
Results may differ from the reference program's by a relative error of at most 0.0003.
Values sent between devices are 32-bit elements; how exact they have to be, the bound alone decides.
No kernel may reach another device: no remote copies, remote signals or barrier semaphores. Data moves between devices by JAX's collectives and lax.ppermute only.
A program may use at most 64 MiB of HBM per device.

```python
import math
import jax
import jax.numpy as jnp
import numpy as np
from jax import lax

P_SIZE = 2048
CAP = 2048
G = 256
MOST = 16
N = 65536


def touch_ends(drawn, rng, low, largest):
    dims = drawn.shape
    place = [jax.random.randint(jax.random.fold_in(rng, axis), (), 0, dims[axis]) for axis in range(len(dims))]
    drawn = drawn.at[tuple(place)].set(low)
    longest = dims.index(max(dims))
    place[longest] = (place[longest] + 1) % dims[longest]
    return drawn.at[tuple(place)].set(largest)


def block_levels(rng, extent, split, smallest, high):
    def one(axis_at, shards_of):
        steps = jax.random.uniform(jax.random.fold_in(jax.random.fold_in(rng, 6), axis_at), (shards_of,), jnp.float32, smallest / len(split), high / len(split))
        return jnp.repeat(jnp.exp(steps), extent[axis_at] // shards_of).reshape((-1,) + (1,) * (len(extent) - axis_at - 1))

    gain = one(*split[0])
    for cut in split[1:]:
        gain = gain * one(*cut)
    return gain


def shared_out(key, own, number, rows, amount, top, most, skew):
    order = jax.random.permutation(key, amount)
    crowded, usual = portions_of(amount, rows * top, most, skew, True), portions_of(amount, rows * top, most, skew, False)
    places = jnp.arange(amount)

    def named(tallies, offset_by):
        used = int((tallies > 0).sum())
        fixed = max(1, used // 4)
        moved = fixed + (places - fixed + offset_by * (used - fixed)) % max(1, amount - fixed)
        return jnp.zeros((amount,), jnp.int32).at[order[jnp.where(places < fixed, places, moved)]].set(jnp.asarray(tallies, jnp.int32))

    tallies = jnp.where(number % 4 == 0, named(crowded, number // 4), named(usual, number - number // 4 - 1))
    mixed = jax.random.permutation(jax.random.fold_in(own, 3), amount)
    source_of, taker = mixed[0:amount // 2 * 2:2], mixed[1:amount // 2 * 2:2]
    room = jnp.minimum(tallies[source_of] - 1, most - tallies[taker]) // 2
    room = jnp.where((source_of == order[0]) | (taker == order[0]) | (tallies[taker] == 0), 0, jnp.maximum(room, 0))
    moved = jax.random.randint(jax.random.fold_in(own, 4), (amount // 2,), 0, 1 << 20) % (room + 1)
    tallies = tallies.at[source_of].add(-moved).at[taker].add(moved)
    members = jnp.searchsorted(jnp.cumsum(tallies), jnp.arange(rows * top), side="right").astype(jnp.int32)
    grid = members.reshape(top, rows).T
    grid = grid[jax.random.permutation(jax.random.fold_in(own, 1), rows)]
    offset_by = jax.random.randint(jax.random.fold_in(own, 2), (rows, 1), 0, top)
    return jnp.take_along_axis(grid, (jnp.arange(top)[None, :] + offset_by) % top, axis=1)


def portions_of(number_of, total, reach, slope, full):
    weights = [(1 << 20) // math.isqrt(grade ** slope) + 1 for grade in range(1, number_of + 1)]
    largest = reach if full else min(reach, max(-(-total // number_of), total * weights[0] // sum(weights)))
    least = 1 if total - largest >= number_of - 1 else 0
    counts, spare = [largest] + [least] * (number_of - 1), total - largest - least * (number_of - 1)
    while spare > 0:
        movable = [i for i in range(1, number_of) if counts[i] < largest] or [i for i in range(1, number_of) if counts[i] < reach]
        pool, left = sum([weights[i] for i in movable]), spare
        for i in movable:
            extra = min(reach - counts[i], max(1, left * weights[i] // pool), spare)
            counts[i] = counts[i] + extra
            spare = spare - extra
    return np.array(counts)


def noise(rng, shape, spread, limit, cuts=(), kind=jnp.bfloat16):
    factor_of = block_levels(rng, shape, cuts, -0.22, 0.18) if cuts else 1.0
    result = jax.random.normal(rng, shape, jnp.float32) * spread * factor_of
    return jnp.minimum(jnp.maximum(result, -limit), limit).astype(kind)


def setup_inputs(seed: int = 0) -> dict:
    keys = jax.random.split(jax.random.key(seed), 7)
    positions = noise(keys[0], (3, N), 1.0, 6.0, ((1, 32),), jnp.float32)
    velocities = noise(keys[1], (3, N), 1.0, 6.0, ((1, 32),), jnp.float32)
    masses = jnp.clip(jnp.exp(math.log(4.0) - 2.7725887 * jax.random.uniform(keys[2], (N,), jnp.float32) ** block_levels(keys[2], (N,), ((0, 32),), -0.2, 0.2)), 0.25, 4.0)
    labels_keys = jax.random.split(jax.random.fold_in(keys[3], 1), N // P_SIZE)
    labels_turns = jax.random.permutation(jax.random.fold_in(keys[3], 3), N // P_SIZE)
    labels = jax.vmap(lambda own, number: shared_out(jax.random.fold_in(keys[3], 2), own, number, P_SIZE, G, 1, MOST, 3))(labels_keys, labels_turns).reshape((N, 1))
    owner_slot = jax.random.permutation(keys[4], G).astype(jnp.int32)
    group_cap = touch_ends(jax.random.randint(keys[5], (G,), CAP // 4, 2 * CAP), jax.random.fold_in(keys[5], 1), CAP // 4, (2 * CAP) - 1).astype(jnp.int32)
    return dict(positions=positions, velocities=velocities, masses=masses, labels=labels, owner_slot=owner_slot, group_cap=group_cap)


softening_sq = 0.0025

def group_potential(block):
    coords = block[0:3]
    weights = block[6]
    width = min(512, CAP)
    column_ids = jnp.arange(CAP, dtype=jnp.int32)

    def row_part(row_start):
        near = lax.dynamic_slice_in_dim(coords, row_start, width, 1)
        row_ids = row_start + jnp.arange(width, dtype=jnp.int32)
        dist_sq = lax.optimization_barrier(jnp.sum((near[:, :, None] - coords[:, None, :]) ** 2, axis=0))
        inverse = jnp.where(row_ids[:, None] == column_ids[None, :], 0.0, lax.rsqrt(dist_sq + softening_sq))
        return -lax.optimization_barrier(jnp.sum(inverse * weights[None, :], axis=1)) / CAP
    starts = jnp.arange(CAP // width, dtype=jnp.int32) * width
    return lax.map(row_part, starts).reshape(CAP)

def reference(positions, velocities, masses, labels, owner_slot, group_cap):
    label_flat = labels[:, 0]
    count_all = label_flat.shape[0]
    ngroups = owner_slot.shape[0]
    order = jnp.argsort(label_flat, stable=True).astype(jnp.int32)
    totals = jax.ops.segment_sum(jnp.ones_like(label_flat), label_flat, ngroups).astype(jnp.int32)
    firsts = jnp.cumsum(totals).astype(jnp.int32) - totals
    sorted_labels = label_flat[order]
    ranks = jnp.zeros_like(label_flat).at[order].set(jnp.arange(count_all, dtype=jnp.int32) - firsts[sorted_labels])
    limits = jnp.minimum(group_cap, CAP)
    kept_counts = jnp.minimum(totals, limits)
    starts = jnp.cumsum(kept_counts).astype(jnp.int32) - kept_counts
    keep = ranks < limits[label_flat]
    compact_index = jnp.where(keep, starts[label_flat] + ranks, -1).astype(jnp.int32)
    slot = jnp.where(keep, label_flat * CAP + ranks, ngroups * CAP).astype(jnp.int32)
    fields = jnp.concatenate([positions, velocities, masses[None, :]], axis=0)
    compact = jnp.zeros((7, ngroups * CAP), jnp.float32).at[:, slot].set(fields, mode='drop')
    compact = jnp.transpose(compact.reshape(7, ngroups, CAP), (1, 0, 2))
    pot = lax.map(group_potential, compact)
    weights = compact[:, 6, :]
    mass_sum = lax.optimization_barrier(jnp.sum(weights, axis=1))
    bulk = lax.optimization_barrier(jnp.sum(weights[:, None, :] * compact[:, 3:6, :], axis=2)) / mass_sum[:, None]
    energy = 0.5 * lax.optimization_barrier(jnp.sum((compact[:, 3:6, :] - bulk[:, :, None]) ** 2, axis=1)) + pot
    safe = jnp.minimum(slot, ngroups * CAP - 1)
    potential = jnp.where(keep, pot.reshape(-1)[safe], 0.0)
    binding = jnp.where(keep, energy.reshape(-1)[safe], 0.0)
    stats = jnp.concatenate([mass_sum[None, :] / CAP, jnp.transpose(bulk)], axis=0)
    catalog = jnp.zeros((4, ngroups), jnp.float32).at[:, owner_slot].set(stats)
    return (compact_index, potential, binding, catalog)
```

```python
import functools

import jax
import jax.numpy as jnp
from jax import lax
from jax.experimental import pallas as pl
from jax.experimental.pallas import tpu as pltpu
from jax.sharding import PartitionSpec as P

CAP = 2048
LANES = 128
CHUNK = 256
CODE = 64
FIELDS = 7
softening_sq = 0.0025
F32 = jnp.float32
BF16 = jnp.bfloat16


def iota(shape, axis):
    return lax.broadcasted_iota(jnp.int32, shape, axis)


def parts_of(x):
    high = x.astype(BF16).astype(F32)
    rest = x - high
    middle = rest.astype(BF16).astype(F32)
    return high, middle, rest - middle


def inverse_column(owner_row, slots):
    groups = owner_row.shape[1]
    ids = iota((groups, groups), 1).astype(F32)
    return jnp.sum(jnp.where(owner_row == slots, ids, 0.0), axis=1, keepdims=True)


def send_kernel(devices, owned, label_ref, owner_ref, pos_ref, vel_ref, mass_ref, out_ref, code_ref):
    count = label_ref.shape[1]
    groups = devices * owned
    span = LANES // owned
    chunks = count // CHUNK
    rows = iota((groups, 1), 0)
    inverse = inverse_column(owner_ref[...], rows)
    upto = (iota((CHUNK, CHUNK), 0) <= iota((CHUNK, CHUNK), 1)).astype(F32).astype(BF16)
    base = jnp.broadcast_to((rows * CODE).astype(F32), (groups, CHUNK))
    owner_ids = iota((devices, 1, 1), 0)
    places = iota((LANES, 1), 0)
    total = jnp.zeros((devices * 8, LANES), F32)
    for chunk in range(chunks):
        cols = slice(chunk * CHUNK, (chunk + 1) * CHUNK)
        label = label_ref[:, cols].astype(F32)
        hit = label == inverse
        prefix = jnp.dot(jnp.where(hit, 1.0, 0.0).astype(BF16), upto, preferred_element_type=F32)
        value = jnp.sum(jnp.where(hit, prefix + base, 0.0), axis=0, keepdims=True)
        base = base + prefix[:, CHUNK - 1 : CHUNK]
        code = value.astype(jnp.int32) - 1
        slot = code // CODE
        rank = code % CODE
        owner = slot // owned
        local = slot % owned
        code_ref[:, cols] = (local * devices + owner) * CODE + rank
        place = local * span + rank
        picked = jnp.where(place == places, 1.0, 0.0).astype(BF16)
        fields = jnp.concatenate(
            [pos_ref[:, cols], vel_ref[:, cols], mass_ref[:, cols], jnp.zeros((1, CHUNK), F32)], axis=0
        )
        mine = owner[None] == owner_ids
        for part in parts_of(fields):
            spread = jnp.where(mine, part[None], 0.0).reshape(devices * 8, CHUNK).astype(BF16)
            total = total + lax.dot_general(
                spread, picked, (((1,), (1,)), ((), ())), preferred_element_type=F32
            )
    for device in range(devices):
        out_ref[device * FIELDS : (device + 1) * FIELDS, :] = total[device * 8 : device * 8 + FIELDS]


def owner_kernel(devices, owned, me_ref, got_ref, owner_ref, cap_ref, out_ref, stats_ref):
    span = LANES // owned
    blocks = devices // 8
    lane = iota((1, LANES), 1)
    offset = lane % span
    segment = lane // span

    def spin(x):
        return jnp.where(offset >= 1, pltpu.roll(x, 1, 1), pltpu.roll(x, LANES + 1 - span, 1))

    field = [got_ref[pl.ds(f, devices, stride=FIELDS), :] for f in range(FIELDS)]
    mass = field[6]
    valid = mass > 0.0

    slots = me_ref[0, 0] * owned + iota((owned, 1), 0)
    limit_col = jnp.sum(
        jnp.where(owner_ref[...] == slots, jnp.minimum(cap_ref[...], CAP).astype(F32), 0.0),
        axis=1,
        keepdims=True,
    )
    limit = jnp.sum(jnp.where(segment == iota((owned, 1), 0), limit_col, 0.0), axis=0, keepdims=True)

    joined = (iota((LANES, 1), 0) // span == segment).astype(F32).astype(BF16)
    counts = jnp.dot(jnp.where(valid, 1.0, 0.0).astype(BF16), joined, preferred_element_type=F32)
    before = (iota((devices, devices), 1) < iota((devices, devices), 0)).astype(F32).astype(BF16)
    prefix = jnp.dot(before, counts.astype(BF16), preferred_element_type=F32)
    kept = jnp.minimum(jnp.sum(counts, axis=0, keepdims=True), limit)
    keep = valid & (prefix + offset.astype(F32) < limit)
    mass = jnp.where(keep, mass, 0.0)

    sums = jnp.concatenate(
        [jnp.sum(x, axis=0, keepdims=True) for x in (mass, mass * field[3], mass * field[4], mass * field[5])]
        + [jnp.zeros((4, LANES), F32)],
        axis=0,
    )
    turned = sums
    for _ in range(span - 1):
        turned = spin(turned)
        sums = sums + turned
    mass_sum = sums[0:1]
    bulk = sums[1:4] / mass_sum
    stats = jnp.concatenate([mass_sum / CAP, bulk, jnp.zeros((4, LANES), F32)], axis=0)
    columns = iota((1, owned), 1)
    table = jnp.zeros((8, owned), F32)
    for group in range(owned):
        table = jnp.where(columns == group, stats[:, group * span : group * span + 1], table)
    stats_ref[...] = table[0:4]

    near = [[x[b * 8 : b * 8 + 8] for b in range(blocks)] for x in (field[0], field[1], field[2], mass)]

    def pair_block(turned, diagonal, one_way, off_diagonal, acc):
        acc = list(acc)
        far_sum = [None] * blocks
        for shift in range(8):
            on_diag = shift in diagonal
            single = shift in one_way
            for b in range(blocks):
                others = list(range(b)) if off_diagonal else []
                if on_diag or single:
                    others.append(b)
                if not others:
                    continue
                far = [turned[k * blocks + b] for k in range(4)]
                if shift:
                    far = [pltpu.roll(x, 8 - shift, 0) for x in far]
                back = None
                for a in others:
                    dx = near[0][a] - far[0]
                    dy = near[1][a] - far[1]
                    dz = near[2][a] - far[2]
                    inverse = lax.rsqrt((dx * dx + dy * dy) + (dz * dz + softening_sq))
                    acc[a] = acc[a] + far[3] * inverse
                    if a == b and single:
                        continue
                    term = near[3][a] * inverse
                    back = term if back is None else back + term
                if back is not None:
                    if shift:
                        back = pltpu.roll(back, shift, 0)
                    far_sum[b] = back if far_sum[b] is None else far_sum[b] + back
        far_sum = [jnp.zeros((8, LANES), F32) if x is None else x for x in far_sum]
        return acc, far_sum

    half = span // 2
    every = tuple(range(8))
    flat = [near[k][b] for k in range(4) for b in range(blocks)]
    zeros = [jnp.zeros((8, LANES), F32)] * blocks

    def turn(diagonal, one_way, _, carry):
        turned, acc, far = carry
        turned = [spin(x) for x in turned]
        acc, extra = pair_block(turned, diagonal, one_way, True, acc)
        far = [spin(x + y) for x, y in zip(far, extra)]
        return turned, acc, far

    carry = (flat, zeros, zeros)
    carry = lax.fori_loop(half + 1, span, functools.partial(turn, (), ()), carry)
    carry = turn((1, 2, 3), (0, 4), 0, carry)
    carry = lax.fori_loop(1, half, functools.partial(turn, every, ()), carry)
    _, acc, far = carry
    acc, extra = pair_block(flat, (1, 2, 3), (4,), True, acc)
    pot = jnp.concatenate([x + (y + z) for x, y, z in zip(acc, far, extra)], axis=0) / -CAP

    wide = functools.partial(jnp.broadcast_to, shape=(devices, LANES))
    more = jnp.where(offset == 3, prefix, wide(kept))
    for axis in range(3):
        more = jnp.where(offset == axis, wide(bulk[axis : axis + 1]), more)
    out_ref[pl.ds(0, devices, stride=2), :] = pot
    out_ref[pl.ds(1, devices, stride=2), :] = more


def final_kernel(
    devices, owned, code_ref, label_ref, owner_ref, vel_ref, got_ref, index_ref, pot_ref, bind_ref
):
    count = code_ref.shape[1]
    groups = devices * owned
    span = LANES // owned
    lane = iota((1, LANES), 1)
    rows = iota((groups, 1), 0)
    inverse = inverse_column(owner_ref[...], (rows % devices) * owned + rows // devices)
    pots = got_ref[pl.ds(0, devices, stride=2), :]
    more = got_ref[pl.ds(1, devices, stride=2), :]
    table = []
    for group in range(owned):
        left = pots if group == 0 else pltpu.roll(pots, LANES - group * span, 1)
        right = pltpu.roll(more, (LANES + span - group * span) % LANES, 1) if group != 1 else more
        table.append(jnp.where(lane < span, left, right))
    table = jnp.transpose(jnp.concatenate(table, axis=0))[0 : 2 * span]
    parts = jnp.concatenate(parts_of(table), axis=0).astype(BF16)
    used = 2 * span
    kept_row = 2 * span - 1
    for chunk in range(count // CHUNK):
        cols = slice(chunk * CHUNK, (chunk + 1) * CHUNK)
        code = code_ref[:, cols]
        rank = code % CODE
        hit = jnp.where(code // CODE == rows, 1.0, 0.0).astype(BF16)
        lower = jnp.where(inverse < label_ref[:, cols].astype(F32), 1.0, 0.0).astype(BF16)
        found = jnp.dot(parts, hit, preferred_element_type=F32)
        found = (found[0:used] + found[used : 2 * used]) + found[2 * used :]
        starts = jnp.dot(parts, lower, preferred_element_type=F32)
        start = starts[kept_row : kept_row + 1] + starts[used + kept_row : used + kept_row + 1]
        pot = jnp.sum(jnp.where(iota((span, 1), 0) == rank, found[0:span], 0.0), axis=0, keepdims=True)
        prefix = found[span + 3 : span + 4]
        kept = found[kept_row : kept_row + 1]
        global_rank = prefix + rank.astype(F32)
        keep = global_rank < kept
        speed = jnp.sum((vel_ref[:, cols] - found[span : span + 3]) ** 2, axis=0, keepdims=True)
        index_ref[:, cols] = jnp.where(keep, (start + global_rank).astype(jnp.int32), -1)
        pot_ref[:, cols] = jnp.where(keep, pot, 0.0)
        bind_ref[:, cols] = jnp.where(keep, 0.5 * speed + pot, 0.0)


def shards(positions, velocities, masses, labels, owner_slot, group_cap):
    count = labels.shape[0]
    groups = owner_slot.shape[0]
    devices = lax.axis_size(("gx", "gy"))
    owned = groups // devices
    label_row = labels.reshape(1, count)
    owner_row = owner_slot.reshape(1, groups)
    cap_row = group_cap.reshape(1, groups)
    me = lax.axis_index(("gx", "gy")).astype(jnp.int32).reshape(1, 1)
    params = pltpu.CompilerParams(vmem_limit_bytes=60 * 1024 * 1024)

    def exchange(x, rows):
        flat = x.reshape(devices * rows * LANES)
        flat = lax.all_to_all(flat, ("gx", "gy"), split_axis=0, concat_axis=0, tiled=True)
        return flat.reshape(devices * rows, LANES)

    outgoing, code = pl.pallas_call(
        functools.partial(send_kernel, devices, owned),
        out_shape=(
            jax.ShapeDtypeStruct((devices * FIELDS, LANES), F32),
            jax.ShapeDtypeStruct((1, count), jnp.int32),
        ),
        compiler_params=params,
        name="send",
    )(label_row, owner_row, positions, velocities, masses.reshape(1, count))
    received = exchange(outgoing, FIELDS)
    answers, catalog = pl.pallas_call(
        functools.partial(owner_kernel, devices, owned),
        out_shape=(
            jax.ShapeDtypeStruct((devices * 2, LANES), F32),
            jax.ShapeDtypeStruct((4, owned), F32),
        ),
        in_specs=[pl.BlockSpec(memory_space=pltpu.SMEM)] + [pl.BlockSpec(memory_space=pltpu.VMEM)] * 3,
        compiler_params=params,
        name="owner",
    )(me, received, owner_row, cap_row)
    returned = exchange(answers, 2)
    index, potential, binding = pl.pallas_call(
        functools.partial(final_kernel, devices, owned),
        out_shape=(
            jax.ShapeDtypeStruct((1, count), jnp.int32),
            jax.ShapeDtypeStruct((1, count), F32),
            jax.ShapeDtypeStruct((1, count), F32),
        ),
        compiler_params=params,
        name="final",
    )(code, label_row, owner_row, velocities, returned)
    return index.reshape(count), potential.reshape(count), binding.reshape(count), catalog


def solution(mesh):
    return jax.shard_map(
        shards,
        mesh=mesh,
        in_specs=(
            P(None, ("gx", "gy")),
            P(None, ("gx", "gy")),
            P(("gx", "gy")),
            P(("gx", "gy"), None),
            P(),
            P(),
        ),
        out_specs=(P(("gx", "gy")), P(("gx", "gy")), P(("gx", "gy")), P(None, ("gx", "gy"))),
        check_vma=False,
    )
```

```python
import functools

import jax
import jax.numpy as jnp
from jax import lax
from jax.experimental import pallas as pl
from jax.experimental.pallas import tpu as pltpu
from jax.sharding import PartitionSpec as P

CAP = 2048
LANES = 128
CHUNK = 256
CODE = 64
FIELDS = 7
softening_sq = 0.0025
F32 = jnp.float32
BF16 = jnp.bfloat16


def iota(shape, axis):
    return lax.broadcasted_iota(jnp.int32, shape, axis)


def parts_of(x):
    high = x.astype(BF16).astype(F32)
    rest = x - high
    middle = rest.astype(BF16).astype(F32)
    return high, middle, rest - middle


def inverse_column(owner_row, slots):
    groups = owner_row.shape[1]
    ids = iota((groups, groups), 1).astype(F32)
    return jnp.sum(jnp.where(owner_row == slots, ids, 0.0), axis=1, keepdims=True)


def send_kernel(
    devices, owned, me_ref, label_hbm, owner_hbm, cap_hbm, pos_hbm, vel_hbm, mass_hbm,
    out_ref, code_ref, limit_ref, owner_out,
    label_ref, owner_ref, cap_ref, pos_ref, vel_ref, mass_ref, parts_ref, hit_ref, spread_ref, block_ref, sems,
):
    count = label_ref.shape[1]
    groups = devices * owned
    span = LANES // owned
    shift = owned.bit_length() - 1
    copies = [
        pltpu.make_async_copy(source, target, sems.at[k])
        for k, (source, target) in enumerate(
            (
                (owner_hbm, owner_ref),
                (label_hbm, label_ref),
                (pos_hbm, pos_ref),
                (vel_hbm, vel_ref),
                (mass_hbm, mass_ref),
                (cap_hbm, cap_ref),
            )
        )
    ]
    for copy in copies:
        copy.start()
    rows = iota((groups, 1), 0)
    upto = (iota((CHUNK, CHUNK), 0) <= iota((CHUNK, CHUNK), 1)).astype(F32).astype(BF16)
    copies[0].wait()
    inverse = inverse_column(owner_ref[...], rows)
    owner_out[...] = owner_ref[...]
    for copy in copies[1:]:
        copy.wait()

    slots = me_ref[0, 0] * owned + iota((owned, 1), 0)
    limit_col = jnp.sum(
        jnp.where(owner_ref[...] == slots, jnp.minimum(cap_ref[...], CAP).astype(F32), 0.0),
        axis=1,
        keepdims=True,
    )
    segment = iota((1, LANES), 1) // span
    limit_ref[...] = jnp.sum(
        jnp.where(segment == iota((owned, 1), 0), limit_col, 0.0), axis=0, keepdims=True
    )

    fields = jnp.concatenate([pos_ref[...], vel_ref[...], mass_ref[...], jnp.zeros((1, count), F32)], axis=0)
    for k, part in enumerate(parts_of(fields)):
        for chunk in range(count // CHUNK):
            parts_ref[chunk * 24 + k * 8 : chunk * 24 + k * 8 + 8, :] = part[:, chunk * CHUNK : (chunk + 1) * CHUNK]
        spread_ref[k * LANES + FIELDS * span : (k + 1) * LANES, :] = jnp.zeros((span, count), BF16)

    base = jnp.broadcast_to((rows * CODE).astype(F32), (groups, LANES))
    ranks = iota((span, 1), 0)
    for chunk in range(count // CHUNK):
        cols = slice(chunk * CHUNK, (chunk + 1) * CHUNK)
        hit = label_ref[:, cols].astype(F32) == inverse
        packed = jnp.where(hit, 1.0, 0.0).astype(BF16)
        hit_ref[:, cols] = packed
        prefix = jnp.dot(packed, upto, preferred_element_type=F32)
        wide = jnp.concatenate([base] * (CHUNK // LANES), axis=1)
        value = jnp.sum(jnp.where(hit, prefix + wide, 0.0), axis=0, keepdims=True)
        base = base + prefix[:, CHUNK - 1 : CHUNK]
        code = value.astype(jnp.int32) - 1
        slot = code >> 6
        rank = code & (CODE - 1)
        code_ref[:, cols] = (((slot & (owned - 1)) * devices + (slot >> shift)) << 6) + rank
        mine = rank == ranks
        for k in range(3):
            for f in range(FIELDS):
                row = parts_ref[pl.ds(chunk * 24 + k * 8 + f, span, stride=0), :]
                spread_ref[k * LANES + f * span : k * LANES + (f + 1) * span, cols] = jnp.where(
                    mine, row, 0.0
                ).astype(BF16)

    found = lax.dot_general(
        hit_ref[...], spread_ref[...], (((1,), (1,)), ((), ())), preferred_element_type=F32
    )
    block_ref[...] = (found[:, 0:LANES] + found[:, LANES : 2 * LANES]) + found[:, 2 * LANES :]
    block = [block_ref[pl.ds(g, devices, stride=owned), :] for g in range(owned)]
    step = owned // 2
    while step:
        upper = (segment & step) != 0
        for low in range(owned):
            if low & step:
                continue
            one, two = block[low], block[low + step]
            block[low] = jnp.where(upper, pltpu.roll(two, step * span, 1), one)
            block[low + step] = jnp.where(upper, two, pltpu.roll(one, LANES - step * span, 1))
        step //= 2
    for f in range(FIELDS):
        out_ref[pl.ds(f, devices, stride=FIELDS), :] = block[f]


def owner_kernel(devices, owned, got_ref, limit_ref, out_ref, stats_ref):
    span = LANES // owned
    blocks = devices // 8
    lane = iota((1, LANES), 1)
    offset = lane % span
    segment = lane // span

    def spin(x):
        return jnp.where(offset >= 1, pltpu.roll(x, 1, 1), pltpu.roll(x, LANES + 1 - span, 1))

    field = [got_ref[pl.ds(f, devices, stride=FIELDS), :] for f in range(FIELDS)]
    mass = field[6]
    valid = mass > 0.0

    limit = limit_ref[...]

    joined = (iota((LANES, 1), 0) // span == segment).astype(F32).astype(BF16)
    counts = jnp.dot(jnp.where(valid, 1.0, 0.0).astype(BF16), joined, preferred_element_type=F32)
    before = (iota((devices, devices), 1) < iota((devices, devices), 0)).astype(F32).astype(BF16)
    prefix = jnp.dot(before, counts.astype(BF16), preferred_element_type=F32)
    kept = jnp.minimum(jnp.sum(counts, axis=0, keepdims=True), limit)
    keep = valid & (prefix + offset.astype(F32) < limit)
    mass = jnp.where(keep, mass, 0.0)

    sums = jnp.concatenate(
        [jnp.sum(x, axis=0, keepdims=True) for x in (mass, mass * field[3], mass * field[4], mass * field[5])]
        + [jnp.zeros((4, LANES), F32)],
        axis=0,
    )
    turned = sums
    for _ in range(span - 1):
        turned = spin(turned)
        sums = sums + turned
    mass_sum = sums[0:1]
    bulk = sums[1:4] / mass_sum
    stats = jnp.concatenate([mass_sum / CAP, bulk, jnp.zeros((4, LANES), F32)], axis=0)
    columns = iota((1, owned), 1)
    table = jnp.zeros((8, owned), F32)
    for group in range(owned):
        table = jnp.where(columns == group, stats[:, group * span : group * span + 1], table)
    stats_ref[...] = table[0:4]

    near = [[x[b * 8 : b * 8 + 8] for b in range(blocks)] for x in (field[0], field[1], field[2], mass)]

    def pair_block(turned, diagonal, one_way, off_diagonal, acc):
        acc = list(acc)
        far_sum = [None] * blocks
        for shift in range(8):
            on_diag = shift in diagonal
            single = shift in one_way
            for b in range(blocks):
                others = list(range(b)) if off_diagonal else []
                if on_diag or single:
                    others.append(b)
                if not others:
                    continue
                far = [turned[k * blocks + b] for k in range(4)]
                if shift:
                    far = [pltpu.roll(x, 8 - shift, 0) for x in far]
                back = None
                for a in others:
                    dx = near[0][a] - far[0]
                    dy = near[1][a] - far[1]
                    dz = near[2][a] - far[2]
                    inverse = lax.rsqrt((dx * dx + dy * dy) + (dz * dz + softening_sq))
                    acc[a] = acc[a] + far[3] * inverse
                    if a == b and single:
                        continue
                    term = near[3][a] * inverse
                    back = term if back is None else back + term
                if back is not None:
                    if shift:
                        back = pltpu.roll(back, shift, 0)
                    far_sum[b] = back if far_sum[b] is None else far_sum[b] + back
        far_sum = [jnp.zeros((8, LANES), F32) if x is None else x for x in far_sum]
        return acc, far_sum

    half = span // 2
    every = tuple(range(8))
    flat = [near[k][b] for k in range(4) for b in range(blocks)]
    zeros = [jnp.zeros((8, LANES), F32)] * blocks

    def turn(diagonal, one_way, _, carry):
        turned, acc, far = carry
        turned = [spin(x) for x in turned]
        acc, extra = pair_block(turned, diagonal, one_way, True, acc)
        far = [spin(x + y) for x, y in zip(far, extra)]
        return turned, acc, far

    def repeat(diagonal, carry):
        if blocks > 4:
            return lax.fori_loop(1, half, functools.partial(turn, diagonal, ()), carry)
        for _ in range(1, half):
            carry = turn(diagonal, (), 0, carry)
        return carry

    carry = repeat((), (flat, zeros, zeros))
    carry = turn((1, 2, 3), (0, 4), 0, carry)
    carry = repeat(every, carry)
    _, acc, far = carry
    acc, extra = pair_block(flat, (1, 2, 3), (4,), True, acc)
    pot = jnp.concatenate([x + (y + z) for x, y, z in zip(acc, far, extra)], axis=0) / -CAP

    wide = functools.partial(jnp.broadcast_to, shape=(devices, LANES))
    more = jnp.where(offset == 3, prefix, wide(kept))
    for axis in range(3):
        more = jnp.where(offset == axis, wide(bulk[axis : axis + 1]), more)
    out_ref[pl.ds(0, devices, stride=2), :] = pot
    out_ref[pl.ds(1, devices, stride=2), :] = more


def final_kernel(
    devices, owned, code_ref, label_ref, owner_ref, vel_ref, got_ref, index_ref, pot_ref, bind_ref
):
    count = code_ref.shape[1]
    groups = devices * owned
    span = LANES // owned
    lane = iota((1, LANES), 1)
    rows = iota((groups, 1), 0)
    inverse = inverse_column(owner_ref[...], (rows % devices) * owned + rows // devices)
    pots = got_ref[pl.ds(0, devices, stride=2), :]
    more = got_ref[pl.ds(1, devices, stride=2), :]
    table = []
    for group in range(owned):
        left = pots if group == 0 else pltpu.roll(pots, LANES - group * span, 1)
        right = pltpu.roll(more, (LANES + span - group * span) % LANES, 1) if group != 1 else more
        table.append(jnp.where(lane < span, left, right))
    table = jnp.transpose(jnp.concatenate(table, axis=0))[0 : 2 * span]
    parts = parts_of(table)
    counted = jnp.concatenate([part[2 * span - 8 :] for part in parts[0:2]], axis=0).astype(BF16)
    parts = jnp.concatenate(parts, axis=0).astype(BF16)
    used = 2 * span
    for chunk in range(count // CHUNK):
        cols = slice(chunk * CHUNK, (chunk + 1) * CHUNK)
        code = code_ref[:, cols]
        rank = code & (CODE - 1)
        hit = jnp.where(code >> 6 == rows, 1.0, 0.0).astype(BF16)
        lower = jnp.where(inverse < label_ref[:, cols].astype(F32), 1.0, 0.0).astype(BF16)
        found = jnp.dot(parts, hit, preferred_element_type=F32)
        found = (found[0:used] + found[used : 2 * used]) + found[2 * used :]
        starts = jnp.dot(counted, lower, preferred_element_type=F32)
        start = starts[7:8] + starts[15:16]
        pot = jnp.sum(jnp.where(iota((span, 1), 0) == rank, found[0:span], 0.0), axis=0, keepdims=True)
        prefix = found[span + 3 : span + 4]
        kept = found[used - 1 : used]
        global_rank = prefix + rank.astype(F32)
        keep = global_rank < kept
        speed = jnp.sum((vel_ref[:, cols] - found[span : span + 3]) ** 2, axis=0, keepdims=True)
        index_ref[:, cols] = jnp.where(keep, (start + global_rank).astype(jnp.int32), -1)
        pot_ref[:, cols] = jnp.where(keep, pot, 0.0)
        bind_ref[:, cols] = jnp.where(keep, 0.5 * speed + pot, 0.0)


def shards(positions, velocities, masses, labels, owner_slot, group_cap):
    count = labels.shape[0]
    groups = owner_slot.shape[0]
    devices = lax.axis_size(("gx", "gy"))
    owned = groups // devices
    label_row = labels.reshape(1, count)
    owner_row = owner_slot.reshape(1, groups)
    cap_row = group_cap.reshape(1, groups)
    me = lax.axis_index(("gx", "gy")).astype(jnp.int32).reshape(1, 1)
    params = pltpu.CompilerParams(vmem_limit_bytes=min(48, 8 * groups // 128) * 1024 * 1024)

    def exchange(x, rows):
        flat = x.reshape(devices * rows * LANES)
        flat = lax.all_to_all(flat, ("gx", "gy"), split_axis=0, concat_axis=0, tiled=True)
        return flat.reshape(devices * rows, LANES)

    outgoing, code, limit, owner_kept = pl.pallas_call(
        functools.partial(send_kernel, devices, owned),
        out_shape=(
            jax.ShapeDtypeStruct((devices * FIELDS, LANES), F32),
            jax.ShapeDtypeStruct((1, count), jnp.int32),
            jax.ShapeDtypeStruct((1, LANES), F32),
            jax.ShapeDtypeStruct((1, groups), jnp.int32),
        ),
        in_specs=[pl.BlockSpec(memory_space=pltpu.SMEM)] + [pl.BlockSpec(memory_space=pltpu.HBM)] * 6,
        scratch_shapes=[
            pltpu.VMEM((1, count), jnp.int32),
            pltpu.VMEM((1, groups), jnp.int32),
            pltpu.VMEM((1, groups), jnp.int32),
            pltpu.VMEM((3, count), F32),
            pltpu.VMEM((3, count), F32),
            pltpu.VMEM((1, count), F32),
            pltpu.VMEM((24 * count // CHUNK, CHUNK), F32),
            pltpu.VMEM((groups, count), BF16),
            pltpu.VMEM((3 * LANES, count), BF16),
            pltpu.VMEM((groups, LANES), F32),
            pltpu.SemaphoreType.DMA((6,)),
        ],
        compiler_params=params,
        name="send",
    )(
        me,
        *(
            pltpu.with_memory_space_constraint(x, pltpu.HBM)
            for x in (label_row, owner_row, cap_row, positions, velocities, masses.reshape(1, count))
        ),
    )
    received = exchange(outgoing, FIELDS)
    answers, catalog = pl.pallas_call(
        functools.partial(owner_kernel, devices, owned),
        out_shape=(
            jax.ShapeDtypeStruct((devices * 2, LANES), F32),
            jax.ShapeDtypeStruct((4, owned), F32),
        ),
        compiler_params=params,
        name="owner",
    )(received, limit)
    returned = exchange(answers, 2)
    index, potential, binding = pl.pallas_call(
        functools.partial(final_kernel, devices, owned),
        out_shape=(
            jax.ShapeDtypeStruct((1, count), jnp.int32),
            jax.ShapeDtypeStruct((1, count), F32),
            jax.ShapeDtypeStruct((1, count), F32),
        ),
        compiler_params=params,
        name="final",
    )(code, label_row, owner_kept, velocities, returned)
    return index.reshape(count), potential.reshape(count), binding.reshape(count), catalog


def solution(mesh):
    return jax.shard_map(
        shards,
        mesh=mesh,
        in_specs=(
            P(None, ("gx", "gy")),
            P(None, ("gx", "gy")),
            P(("gx", "gy")),
            P(("gx", "gy"), None),
            P(),
            P(),
        ),
        out_specs=(P(("gx", "gy")), P(("gx", "gy")), P(("gx", "gy")), P(None, ("gx", "gy"))),
        check_vma=False,
    )
```

```python
import functools

import jax
import jax.numpy as jnp
from jax import lax
from jax.experimental import pallas as pl
from jax.experimental.pallas import tpu as pltpu
from jax.sharding import PartitionSpec as P

CAP = 2048
LANES = 128
CHUNK = 256
FIELDS = 7
softening_sq = 0.0025
F32 = jnp.float32
BF16 = jnp.bfloat16


def iota(shape, axis):
    return lax.broadcasted_iota(jnp.int32, shape, axis)


def parts_of(x):
    high = x.astype(BF16).astype(F32)
    rest = x - high
    middle = rest.astype(BF16).astype(F32)
    return high, middle, rest - middle


def inverse_column(owner_row, slots):
    groups = owner_row.shape[1]
    ids = iota((groups, groups), 1).astype(F32)
    return jnp.sum(jnp.where(owner_row == slots, ids, 0.0), axis=1, keepdims=True)


def send_kernel(
    devices, owned, me_ref, label_hbm, owner_hbm, cap_hbm, pos_hbm, vel_hbm, mass_hbm,
    out_ref, rank_ref, limit_ref, hit_ref, order_ref,
    label_ref, owner_ref, cap_ref, pos_ref, vel_ref, mass_ref, parts_ref, spread_ref, sems,
):
    count = label_ref.shape[1]
    groups = devices * owned
    span = LANES // owned
    chunks = count // CHUNK
    copies = [
        pltpu.make_async_copy(source, target, sems.at[k])
        for k, (source, target) in enumerate(
            (
                (owner_hbm, owner_ref),
                (label_hbm, label_ref),
                (pos_hbm, pos_ref),
                (vel_hbm, vel_ref),
                (mass_hbm, mass_ref),
                (cap_hbm, cap_ref),
            )
        )
    ]
    for copy in copies:
        copy.start()
    rows = iota((groups, 1), 0)
    upto = (iota((CHUNK, CHUNK), 0) <= iota((CHUNK, CHUNK), 1)).astype(F32).astype(BF16)
    copies[0].wait()
    inverse = inverse_column(owner_ref[...], (rows % devices) * owned + rows // devices)
    for copy in copies[1:]:
        copy.wait()

    kind = BF16 if groups <= 256 else F32
    name = jnp.broadcast_to(inverse, (groups, CHUNK)).astype(kind)
    for chunk in range(chunks):
        cols = slice(chunk * CHUNK, (chunk + 1) * CHUNK)
        label = label_ref[:, cols].astype(F32).astype(kind)
        hit_ref[:, cols] = jnp.where(label == name, jnp.ones((), kind), jnp.zeros((), kind)).astype(BF16)
    prefixes = [jnp.dot(hit_ref[:, chunk * CHUNK : (chunk + 1) * CHUNK], upto, preferred_element_type=F32) for chunk in range(chunks)]

    fields = jnp.concatenate([pos_ref[...], vel_ref[...], mass_ref[...], jnp.zeros((1, count), F32)], axis=0)
    for k, part in enumerate(parts_of(fields)):
        for chunk in range(chunks):
            parts_ref[chunk * 24 + k * 8 : chunk * 24 + k * 8 + 8, :] = part[:, chunk * CHUNK : (chunk + 1) * CHUNK]

    base = jnp.zeros((groups, CHUNK), BF16)
    ranks = iota((span, 1), 0)
    for chunk in range(chunks):
        cols = slice(chunk * CHUNK, (chunk + 1) * CHUNK)
        prefix = prefixes[chunk]
        mine = (prefix.astype(BF16) + base) * hit_ref[:, cols]
        base = base + jnp.broadcast_to(prefix[:, CHUNK - 1 : CHUNK], (groups, CHUNK)).astype(BF16)
        while mine.shape[0] > 16:
            half = mine.shape[0] // 2
            mine = mine[0:half] + mine[half:]
        rank = jnp.sum(mine.astype(F32), axis=0, keepdims=True).astype(jnp.int32) - 1
        rank_ref[:, cols] = rank
        here = rank == ranks
        for k in range(3):
            for f in range(FIELDS):
                row = parts_ref[pl.ds(chunk * 24 + k * 8 + f, span, stride=0), :]
                first = (k * FIELDS + f) * span
                spread_ref[first : first + span, cols] = jnp.where(
                    here, row, 0.0
                ).astype(BF16)

    found = lax.dot_general(
        spread_ref[...], hit_ref[...], (((1,), (1,)), ((), ())), preferred_element_type=F32
    )
    size = FIELDS * span
    found = (found[0:size] + found[size : 2 * size]) + found[2 * size :]
    found = jnp.concatenate([found, jnp.zeros((LANES - size, groups), F32)], axis=0)

    slots = me_ref[0, 0] * owned + iota((owned, 1), 0)
    limit_col = jnp.sum(
        jnp.where(owner_ref[...] == slots, jnp.minimum(cap_ref[...], CAP).astype(F32), 0.0),
        axis=1,
        keepdims=True,
    )
    segment = iota((1, LANES), 1) // span
    limit_ref[...] = jnp.sum(
        jnp.where(segment == iota((owned, 1), 0), limit_col, 0.0), axis=0, keepdims=True
    )
    inverse_row = jnp.sum(jnp.where(rows == iota((1, groups), 1), inverse, 0.0), axis=0, keepdims=True)
    order_ref[...] = jnp.where(inverse < inverse_row, 1.0, 0.0).astype(BF16)

    found = jnp.transpose(found)
    block = [found[g * devices : (g + 1) * devices] for g in range(owned)]
    step = owned // 2
    while step:
        upper = (segment & step) != 0
        for low in range(owned):
            if low & step:
                continue
            one, two = block[low], block[low + step]
            block[low] = jnp.where(upper, pltpu.roll(two, step * span, 1), one)
            block[low + step] = jnp.where(upper, two, pltpu.roll(one, LANES - step * span, 1))
        step //= 2
    for f in range(FIELDS):
        out_ref[pl.ds(f, devices, stride=FIELDS), :] = block[f]


def owner_kernel(devices, owned, got_ref, limit_ref, out_ref, stats_ref, far_ref):
    span = LANES // owned
    blocks = devices // 8
    lane = iota((1, LANES), 1)
    offset = lane % span
    segment = lane // span

    def spin(x):
        return jnp.where(offset >= 1, pltpu.roll(x, 1, 1), pltpu.roll(x, LANES + 1 - span, 1))

    field = [got_ref[pl.ds(f, devices, stride=FIELDS), :] for f in range(FIELDS)]
    mass = field[6]
    valid = mass > 0.0

    limit = limit_ref[...]

    joined = (iota((LANES, 1), 0) // span == segment).astype(F32).astype(BF16)
    counts = jnp.dot(jnp.where(valid, 1.0, 0.0).astype(BF16), joined, preferred_element_type=F32)
    before = (iota((devices, devices), 1) < iota((devices, devices), 0)).astype(F32).astype(BF16)
    prefix = jnp.dot(before, counts.astype(BF16), preferred_element_type=F32)
    kept = jnp.minimum(jnp.sum(counts, axis=0, keepdims=True), limit)
    keep = valid & (prefix + offset.astype(F32) < limit)
    mass = jnp.where(keep, mass, 0.0)

    sums = jnp.concatenate(
        [jnp.sum(x, axis=0, keepdims=True) for x in (mass, mass * field[3], mass * field[4], mass * field[5])]
        + [jnp.zeros((4, LANES), F32)],
        axis=0,
    )
    turned = sums
    for _ in range(span - 1):
        turned = spin(turned)
        sums = sums + turned
    mass_sum = sums[0:1]
    bulk = sums[1:4] / mass_sum
    stats = jnp.concatenate([mass_sum / CAP, bulk, jnp.zeros((4, LANES), F32)], axis=0)
    columns = iota((1, owned), 1)
    table = jnp.zeros((8, owned), F32)
    for group in range(owned):
        table = jnp.where(columns == group, stats[:, group * span : group * span + 1], table)
    stats_ref[...] = table[0:4]

    near = [[x[b * 8 : b * 8 + 8] for b in range(blocks)] for x in (field[0], field[1], field[2], mass)]

    def pair_block(turned, diagonal, one_way, slot, acc):
        acc = list(acc)
        far_sum = [None] * blocks
        for k in range(4 * blocks):
            far_ref[slot, k * 16 : k * 16 + 8, :] = turned[k]
            far_ref[slot, k * 16 + 8 : k * 16 + 16, :] = turned[k]
        for shift in range(8):
            on_diag = shift in diagonal
            single = shift in one_way
            for b in range(blocks):
                others = list(range(b))
                if on_diag or single:
                    others.append(b)
                if not others:
                    continue
                far = [turned[k * blocks + b] for k in range(4)]
                if shift:
                    starts = [(k * blocks + b) * 16 + shift for k in range(4)]
                    far = [far_ref[slot, start : start + 8, :] for start in starts]
                back = None
                for a in others:
                    dx = near[0][a] - far[0]
                    dy = near[1][a] - far[1]
                    dz = near[2][a] - far[2]
                    inverse = lax.rsqrt((dx * dx + dy * dy) + (dz * dz + softening_sq))
                    acc[a] = acc[a] + far[3] * inverse
                    if a == b and single:
                        continue
                    term = near[3][a] * inverse
                    back = term if back is None else back + term
                if back is not None:
                    if shift:
                        back = pltpu.roll(back, shift, 0)
                    far_sum[b] = back if far_sum[b] is None else far_sum[b] + back
        far_sum = [jnp.zeros((8, LANES), F32) if x is None else x for x in far_sum]
        return acc, far_sum

    half = span // 2
    every = tuple(range(8))
    flat = [near[k][b] for k in range(4) for b in range(blocks)]
    zeros = [jnp.zeros((8, LANES), F32)] * blocks

    def turn(diagonal, one_way, step, carry):
        turned, acc, far = carry
        turned = [spin(x) for x in turned]
        acc, extra = pair_block(turned, diagonal, one_way, step % 2, acc)
        far = [spin(x + y) for x, y in zip(far, extra)]
        return turned, acc, far

    def repeat(diagonal, carry):
        if blocks > 4:
            return lax.fori_loop(1, half, functools.partial(turn, diagonal, ()), carry)
        for step in range(1, half):
            carry = turn(diagonal, (), step, carry)
        return carry

    carry = repeat((), (flat, zeros, zeros))
    carry = turn((1, 2, 3), (0, 4), 0, carry)
    carry = repeat(every, carry)
    _, acc, far = carry
    acc, extra = pair_block(flat, (1, 2, 3), (4,), 0, acc)
    pot = jnp.concatenate([x + (y + z) for x, y, z in zip(acc, far, extra)], axis=0) / -CAP

    wide = functools.partial(jnp.broadcast_to, shape=(devices, LANES))
    more = jnp.where(offset == 3, prefix, wide(kept))
    for axis in range(3):
        more = jnp.where(offset == axis, wide(bulk[axis : axis + 1]), more)
    out_ref[pl.ds(0, devices, stride=2), :] = pot
    out_ref[pl.ds(1, devices, stride=2), :] = more


def final_kernel(devices, owned, rank_ref, hit_ref, order_ref, vel_ref, got_ref, index_ref, pot_ref, bind_ref):
    count = rank_ref.shape[1]
    groups = devices * owned
    span = LANES // owned
    used = 2 * span
    lane = iota((1, LANES), 1)
    pots = got_ref[pl.ds(0, devices, stride=2), :]
    more = got_ref[pl.ds(1, devices, stride=2), :]
    table = []
    for group in range(owned):
        left = pots if group == 0 else pltpu.roll(pots, LANES - group * span, 1)
        right = pltpu.roll(more, (LANES + span - group * span) % LANES, 1) if group != 1 else more
        table.append(jnp.where(lane < span, left, right))
    table = jnp.transpose(jnp.concatenate(table, axis=0))[0:used]
    parts = parts_of(table)
    counted = jnp.concatenate([part[used - 8 :] for part in parts[0:2]], axis=0).astype(BF16)
    starts = jnp.dot(counted, order_ref[...], preferred_element_type=F32)
    starts = jnp.broadcast_to(starts[7:8] + starts[15:16], (8, groups))
    parts = jnp.concatenate([*parts, *parts_of(starts)], axis=0).astype(BF16)
    for chunk in range(count // CHUNK):
        cols = slice(chunk * CHUNK, (chunk + 1) * CHUNK)
        rank = rank_ref[:, cols]
        found = jnp.dot(parts, hit_ref[:, cols], preferred_element_type=F32)
        start = (found[3 * used : 3 * used + 1] + found[3 * used + 8 : 3 * used + 9]) + found[
            3 * used + 16 : 3 * used + 17
        ]
        found = (found[0:used] + found[used : 2 * used]) + found[2 * used : 3 * used]
        pot = jnp.sum(jnp.where(iota((span, 1), 0) == rank, found[0:span], 0.0), axis=0, keepdims=True)
        prefix = found[span + 3 : span + 4]
        kept = found[used - 1 : used]
        global_rank = prefix + rank.astype(F32)
        keep = global_rank < kept
        speed = jnp.sum((vel_ref[:, cols] - found[span : span + 3]) ** 2, axis=0, keepdims=True)
        index_ref[:, cols] = jnp.where(keep, (start + global_rank).astype(jnp.int32), -1)
        pot_ref[:, cols] = jnp.where(keep, pot, 0.0)
        bind_ref[:, cols] = jnp.where(keep, 0.5 * speed + pot, 0.0)


def shards(positions, velocities, masses, labels, owner_slot, group_cap):
    count = labels.shape[0]
    groups = owner_slot.shape[0]
    devices = lax.axis_size(("gx", "gy"))
    owned = groups // devices
    label_row = labels.reshape(1, count)
    owner_row = owner_slot.reshape(1, groups)
    cap_row = group_cap.reshape(1, groups)
    me = lax.axis_index(("gx", "gy")).astype(jnp.int32).reshape(1, 1)
    params = pltpu.CompilerParams(vmem_limit_bytes=min(48, 8 * groups // 128) * 1024 * 1024)

    def exchange(x, rows):
        flat = x.reshape(devices * rows * LANES)
        flat = lax.all_to_all(flat, ("gx", "gy"), split_axis=0, concat_axis=0, tiled=True)
        return flat.reshape(devices * rows, LANES)

    outgoing, rank, limit, hit, order = pl.pallas_call(
        functools.partial(send_kernel, devices, owned),
        out_shape=(
            jax.ShapeDtypeStruct((devices * FIELDS, LANES), F32),
            jax.ShapeDtypeStruct((1, count), jnp.int32),
            jax.ShapeDtypeStruct((1, LANES), F32),
            jax.ShapeDtypeStruct((groups, count), BF16),
            jax.ShapeDtypeStruct((groups, groups), BF16),
        ),
        in_specs=[pl.BlockSpec(memory_space=pltpu.SMEM)] + [pl.BlockSpec(memory_space=pltpu.HBM)] * 6,
        scratch_shapes=[
            pltpu.VMEM((1, count), jnp.int32),
            pltpu.VMEM((1, groups), jnp.int32),
            pltpu.VMEM((1, groups), jnp.int32),
            pltpu.VMEM((3, count), F32),
            pltpu.VMEM((3, count), F32),
            pltpu.VMEM((1, count), F32),
            pltpu.VMEM((24 * count // CHUNK, CHUNK), F32),
            pltpu.VMEM((3 * FIELDS * LANES // owned, count), BF16),
            pltpu.SemaphoreType.DMA((6,)),
        ],
        compiler_params=params,
        name="send",
    )(
        me,
        *(
            pltpu.with_memory_space_constraint(x, pltpu.HBM)
            for x in (label_row, owner_row, cap_row, positions, velocities, masses.reshape(1, count))
        ),
    )
    received = exchange(outgoing, FIELDS)
    answers, catalog = pl.pallas_call(
        functools.partial(owner_kernel, devices, owned),
        out_shape=(
            jax.ShapeDtypeStruct((devices * 2, LANES), F32),
            jax.ShapeDtypeStruct((4, owned), F32),
        ),
        scratch_shapes=[pltpu.VMEM((2, devices * 8, LANES), F32)],
        compiler_params=params,
        name="owner",
    )(received, limit)
    returned = exchange(answers, 2)
    index, potential, binding = pl.pallas_call(
        functools.partial(final_kernel, devices, owned),
        out_shape=(
            jax.ShapeDtypeStruct((1, count), jnp.int32),
            jax.ShapeDtypeStruct((1, count), F32),
            jax.ShapeDtypeStruct((1, count), F32),
        ),
        compiler_params=params,
        name="final",
    )(rank, hit, order, velocities, returned)
    return index.reshape(count), potential.reshape(count), binding.reshape(count), catalog


def solution(mesh):
    return jax.shard_map(
        shards,
        mesh=mesh,
        in_specs=(
            P(None, ("gx", "gy")),
            P(None, ("gx", "gy")),
            P(("gx", "gy")),
            P(("gx", "gy"), None),
            P(),
            P(),
        ),
        out_specs=(P(("gx", "gy")), P(("gx", "gy")), P(("gx", "gy")), P(None, ("gx", "gy"))),
        check_vma=False,
    )
```

```python
import functools

import jax
import jax.numpy as jnp
from jax import lax
from jax.experimental import pallas as pl
from jax.experimental.pallas import tpu as pltpu
from jax.sharding import PartitionSpec as P

CAP = 2048
LANES = 128
CHUNK = 256
FIELDS = 7
softening_sq = 0.0025
F32 = jnp.float32
BF16 = jnp.bfloat16


def iota(shape, axis):
    return lax.broadcasted_iota(jnp.int32, shape, axis)


def parts_of(x):
    high = x.astype(BF16).astype(F32)
    rest = x - high
    middle = rest.astype(BF16).astype(F32)
    return high, middle, rest - middle


def inverse_column(owner_row, slots):
    groups = owner_row.shape[1]
    ids = iota((groups, groups), 1).astype(F32)
    return jnp.sum(jnp.where(owner_row == slots, ids, 0.0), axis=1, keepdims=True)


def send_kernel(
    devices, owned, me_ref, label_hbm, owner_hbm, cap_hbm, pos_hbm, vel_hbm, mass_hbm,
    out_ref, rank_ref, limit_ref, hit_out, order_ref,
    label_ref, owner_ref, cap_ref, pos_ref, vel_ref, mass_ref, parts_ref, hit_ref, spread_ref, sems,
):
    count = label_ref.shape[1]
    groups = devices * owned
    span = LANES // owned
    chunks = count // CHUNK
    copies = [
        pltpu.make_async_copy(source, target, sems.at[k])
        for k, (source, target) in enumerate(
            (
                (owner_hbm, owner_ref),
                (label_hbm, label_ref),
                (pos_hbm, pos_ref),
                (vel_hbm, vel_ref),
                (mass_hbm, mass_ref),
                (cap_hbm, cap_ref),
            )
        )
    ]
    for copy in copies:
        copy.start()
    rows = iota((groups, 1), 0)
    upto = (iota((CHUNK, CHUNK), 0) <= iota((CHUNK, CHUNK), 1)).astype(F32).astype(BF16)
    copies[0].wait()
    inverse = inverse_column(owner_ref[...], (rows % devices) * owned + rows // devices)
    for copy in copies[1:]:
        copy.wait()

    kind = BF16 if groups <= 256 else F32
    name = jnp.broadcast_to(inverse, (groups, CHUNK)).astype(kind)
    for chunk in range(chunks):
        cols = slice(chunk * CHUNK, (chunk + 1) * CHUNK)
        label = jnp.broadcast_to(label_ref[:, cols].astype(F32), (16, CHUNK)).astype(kind)
        for row in range(0, groups, 16):
            here = slice(row, row + 16)
            hit = jnp.where(label == name[here], jnp.ones((), kind), jnp.zeros((), kind)).astype(BF16)
            hit_ref[here, cols] = hit
            hit_out[here, cols] = hit
    prefixes = [jnp.dot(hit_ref[:, chunk * CHUNK : (chunk + 1) * CHUNK], upto, preferred_element_type=F32) for chunk in range(chunks)]

    fields = jnp.concatenate([pos_ref[...], vel_ref[...], mass_ref[...], jnp.zeros((1, count), F32)], axis=0)
    for k, part in enumerate(parts_of(fields)):
        for chunk in range(chunks):
            parts_ref[chunk * 24 + k * 8 : chunk * 24 + k * 8 + 8, :] = part[:, chunk * CHUNK : (chunk + 1) * CHUNK]

    base = jnp.zeros((groups, CHUNK), BF16)
    ranks = iota((span, 1), 0).astype(F32)
    for chunk in range(chunks):
        cols = slice(chunk * CHUNK, (chunk + 1) * CHUNK)
        prefix = prefixes[chunk]
        mine = (prefix.astype(BF16) + base) * hit_ref[:, cols]
        base = base + jnp.broadcast_to(prefix[:, CHUNK - 1 : CHUNK], (groups, CHUNK)).astype(BF16)
        while mine.shape[0] > 16:
            half = mine.shape[0] // 2
            mine = mine[0:half] + mine[half:]
        rank = jnp.sum(mine.astype(F32), axis=0, keepdims=True) - 1.0
        rank_ref[:, cols] = rank.astype(jnp.int32)
        here = rank == ranks
        for k in range(3):
            for f in range(FIELDS):
                row = parts_ref[pl.ds(chunk * 24 + k * 8 + f, span, stride=0), :]
                first = (k * FIELDS + f) * span
                spread_ref[first : first + span, cols] = jnp.where(
                    here, row, 0.0
                ).astype(BF16)

    found = lax.dot_general(
        spread_ref[...], hit_ref[...], (((1,), (1,)), ((), ())), preferred_element_type=F32
    )
    size = FIELDS * span
    found = (found[0:size] + found[size : 2 * size]) + found[2 * size :]
    slots = me_ref[0, 0] * owned + iota((owned, 1), 0)
    limit_col = jnp.sum(
        jnp.where(owner_ref[...] == slots, jnp.minimum(cap_ref[...], CAP).astype(F32), 0.0),
        axis=1,
        keepdims=True,
    )
    segment = iota((1, LANES), 1) // span
    limit_ref[...] = jnp.sum(
        jnp.where(segment == iota((owned, 1), 0), limit_col, 0.0), axis=0, keepdims=True
    )
    inverse_row = jnp.sum(jnp.where(rows == iota((1, groups), 1), inverse, 0.0), axis=0, keepdims=True)
    order_ref[...] = jnp.where(inverse < inverse_row, 1.0, 0.0).astype(BF16)

    block = max(1, LANES // devices)
    upper = iota((1, LANES), 1) // devices
    tiles = []
    for tile in range(owned // block):
        lanes = slice(tile * LANES, (tile + 1) * LANES)
        piece = [found[f * span : (f + 1) * span, lanes] for f in range(FIELDS)]
        piece += [jnp.zeros((span, LANES), F32)] * (-FIELDS % block)
        step = block // 2
        while step:
            far = (upper & step) != 0
            for low in range(len(piece)):
                if low & step:
                    continue
                one, two = piece[low], piece[low + step]
                piece[low] = jnp.where(far, pltpu.roll(two, step * devices, 1), one)
                piece[low + step] = jnp.where(far, two, pltpu.roll(one, LANES - step * devices, 1))
            step //= 2
        tiles.append(piece)
    for first in range(0, FIELDS, block):
        turned = jnp.transpose(
            jnp.concatenate([piece[first + k] for piece in tiles for k in range(block)], axis=0)
        )
        for f in range(first, min(first + block, FIELDS)):
            low = (f - first) * devices
            out_ref[pl.ds(f, devices, stride=FIELDS), :] = turned[low : low + devices]


def owner_kernel(devices, owned, got_ref, limit_ref, out_ref, stats_ref, far_ref):
    span = LANES // owned
    blocks = devices // 8
    lane = iota((1, LANES), 1)
    offset = lane % span
    segment = lane // span

    def spin(x):
        return jnp.where(offset >= 1, pltpu.roll(x, 1, 1), pltpu.roll(x, LANES + 1 - span, 1))

    field = [got_ref[pl.ds(f, devices, stride=FIELDS), :] for f in range(FIELDS)]
    mass = field[6]
    valid = mass > 0.0

    limit = limit_ref[...]

    joined = (iota((LANES, 1), 0) // span == segment).astype(F32).astype(BF16)
    counts = jnp.dot(jnp.where(valid, 1.0, 0.0).astype(BF16), joined, preferred_element_type=F32)
    before = (iota((devices, devices), 1) < iota((devices, devices), 0)).astype(F32).astype(BF16)
    prefix = jnp.dot(before, counts.astype(BF16), preferred_element_type=F32)
    kept = jnp.minimum(jnp.sum(counts, axis=0, keepdims=True), limit)
    keep = valid & (prefix + offset.astype(F32) < limit)
    mass = jnp.where(keep, mass, 0.0)

    sums = jnp.concatenate(
        [jnp.sum(x, axis=0, keepdims=True) for x in (mass, mass * field[3], mass * field[4], mass * field[5])]
        + [jnp.zeros((4, LANES), F32)],
        axis=0,
    )
    turned = sums
    for _ in range(span - 1):
        turned = spin(turned)
        sums = sums + turned
    mass_sum = sums[0:1]
    bulk = sums[1:4] / mass_sum
    stats = jnp.concatenate([mass_sum / CAP, bulk, jnp.zeros((4, LANES), F32)], axis=0)
    columns = iota((1, owned), 1)
    table = jnp.zeros((8, owned), F32)
    for group in range(owned):
        table = jnp.where(columns == group, stats[:, group * span : group * span + 1], table)
    stats_ref[...] = table[0:4]

    near = [[x[b * 8 : b * 8 + 8] for b in range(blocks)] for x in (field[0], field[1], field[2], mass)]

    def pair_block(turned, diagonal, one_way, slot, acc):
        acc = list(acc)
        far_sum = [None] * blocks
        for k in range(4 * blocks):
            far_ref[slot, k * 16 : k * 16 + 8, :] = turned[k]
            far_ref[slot, k * 16 + 8 : k * 16 + 16, :] = turned[k]
        for shift in range(8):
            on_diag = shift in diagonal
            single = shift in one_way
            for b in range(blocks):
                others = list(range(b))
                if on_diag or single:
                    others.append(b)
                if not others:
                    continue
                far = [turned[k * blocks + b] for k in range(4)]
                if shift:
                    starts = [(k * blocks + b) * 16 + shift for k in range(4)]
                    far = [far_ref[slot, start : start + 8, :] for start in starts]
                back = None
                for a in others:
                    dx = near[0][a] - far[0]
                    dy = near[1][a] - far[1]
                    dz = near[2][a] - far[2]
                    inverse = lax.rsqrt((dx * dx + dy * dy) + (dz * dz + softening_sq))
                    acc[a] = acc[a] + far[3] * inverse
                    if a == b and single:
                        continue
                    term = near[3][a] * inverse
                    back = term if back is None else back + term
                if back is not None:
                    if shift:
                        back = pltpu.roll(back, shift, 0)
                    far_sum[b] = back if far_sum[b] is None else far_sum[b] + back
        far_sum = [jnp.zeros((8, LANES), F32) if x is None else x for x in far_sum]
        return acc, far_sum

    half = span // 2
    every = tuple(range(8))
    flat = [near[k][b] for k in range(4) for b in range(blocks)]
    zeros = [jnp.zeros((8, LANES), F32)] * blocks

    def turn(diagonal, one_way, step, carry):
        turned, acc, far = carry
        turned = [spin(x) for x in turned]
        acc, extra = pair_block(turned, diagonal, one_way, step % 2, acc)
        far = [spin(x + y) for x, y in zip(far, extra)]
        return turned, acc, far

    def repeat(diagonal, carry):
        if blocks > 4:
            return lax.fori_loop(1, half, functools.partial(turn, diagonal, ()), carry)
        for step in range(1, half):
            carry = turn(diagonal, (), step, carry)
        return carry

    carry = repeat((), (flat, zeros, zeros))
    carry = turn((1, 2, 3), (0, 4), 0, carry)
    carry = repeat(every, carry)
    _, acc, far = carry
    acc, extra = pair_block(flat, (1, 2, 3), (4,), 0, acc)
    pot = jnp.concatenate([x + (y + z) for x, y, z in zip(acc, far, extra)], axis=0) / -CAP

    wide = functools.partial(jnp.broadcast_to, shape=(devices, LANES))
    more = jnp.where(offset == 3, prefix, wide(kept))
    for axis in range(3):
        more = jnp.where(offset == axis, wide(bulk[axis : axis + 1]), more)
    out_ref[pl.ds(0, devices, stride=2), :] = pot
    out_ref[pl.ds(1, devices, stride=2), :] = more


def final_kernel(devices, owned, rank_ref, hit_ref, order_ref, vel_ref, got_ref, index_ref, pot_ref, bind_ref):
    count = rank_ref.shape[1]
    groups = devices * owned
    span = LANES // owned
    used = 2 * span
    block = max(1, LANES // devices)
    both = [got_ref[pl.ds(k, devices, stride=2), :] for k in range(2)]
    both += [jnp.zeros((-2 * devices % LANES, LANES), F32)] if 2 * devices % LANES else []
    turned = jnp.transpose(jnp.concatenate(both, axis=0))
    place = iota((1, LANES), 1) // devices
    table = []
    for k in range(2):
        tile, offset = divmod(k * devices, LANES)
        row = []
        for first in range(0, owned, block):
            filled = None
            for j in range(block):
                piece = turned[(first + j) * span : (first + j + 1) * span, tile * LANES : (tile + 1) * LANES]
                shift = (j * devices - offset) % LANES
                piece = pltpu.roll(piece, shift, 1) if shift else piece
                filled = piece if filled is None else jnp.where(place == j, piece, filled)
            row.append(filled)
        table.append(jnp.concatenate(row, axis=1))
    table = jnp.concatenate(table, axis=0)
    parts = parts_of(table)
    counted = jnp.concatenate([part[used - 8 :] for part in parts[0:2]], axis=0).astype(BF16)
    starts = jnp.dot(counted, order_ref[...], preferred_element_type=F32)
    starts = jnp.broadcast_to(starts[7:8] + starts[15:16], (8, groups))
    parts = jnp.concatenate([*parts, *parts_of(starts)], axis=0).astype(BF16)
    for chunk in range(count // CHUNK):
        cols = slice(chunk * CHUNK, (chunk + 1) * CHUNK)
        rank = rank_ref[:, cols]
        found = jnp.dot(parts, hit_ref[:, cols], preferred_element_type=F32)
        start = (found[3 * used : 3 * used + 1] + found[3 * used + 8 : 3 * used + 9]) + found[
            3 * used + 16 : 3 * used + 17
        ]
        found = (found[0:used] + found[used : 2 * used]) + found[2 * used : 3 * used]
        pot = jnp.sum(jnp.where(iota((span, 1), 0) == rank, found[0:span], 0.0), axis=0, keepdims=True)
        prefix = found[span + 3 : span + 4]
        kept = found[used - 1 : used]
        global_rank = prefix + rank.astype(F32)
        keep = global_rank < kept
        speed = jnp.sum((vel_ref[:, cols] - found[span : span + 3]) ** 2, axis=0, keepdims=True)
        index_ref[:, cols] = jnp.where(keep, (start + global_rank).astype(jnp.int32), -1)
        pot_ref[:, cols] = jnp.where(keep, pot, 0.0)
        bind_ref[:, cols] = jnp.where(keep, 0.5 * speed + pot, 0.0)


def shards(positions, velocities, masses, labels, owner_slot, group_cap):
    count = labels.shape[0]
    groups = owner_slot.shape[0]
    devices = lax.axis_size(("gx", "gy"))
    owned = groups // devices
    label_row = labels.reshape(1, count)
    owner_row = owner_slot.reshape(1, groups)
    cap_row = group_cap.reshape(1, groups)
    me = lax.axis_index(("gx", "gy")).astype(jnp.int32).reshape(1, 1)
    params = pltpu.CompilerParams(vmem_limit_bytes=min(48, 8 * groups // 128) * 1024 * 1024)

    def exchange(x, rows):
        flat = x.reshape(devices * rows * LANES)
        flat = lax.all_to_all(flat, ("gx", "gy"), split_axis=0, concat_axis=0, tiled=True)
        return flat.reshape(devices * rows, LANES)

    outgoing, rank, limit, hit, order = pl.pallas_call(
        functools.partial(send_kernel, devices, owned),
        out_shape=(
            jax.ShapeDtypeStruct((devices * FIELDS, LANES), F32),
            jax.ShapeDtypeStruct((1, count), jnp.int32),
            jax.ShapeDtypeStruct((1, LANES), F32),
            jax.ShapeDtypeStruct((groups, count), BF16),
            jax.ShapeDtypeStruct((groups, groups), BF16),
        ),
        in_specs=[pl.BlockSpec(memory_space=pltpu.SMEM)] + [pl.BlockSpec(memory_space=pltpu.HBM)] * 6,
        scratch_shapes=[
            pltpu.VMEM((1, count), jnp.int32),
            pltpu.VMEM((1, groups), jnp.int32),
            pltpu.VMEM((1, groups), jnp.int32),
            pltpu.VMEM((3, count), F32),
            pltpu.VMEM((3, count), F32),
            pltpu.VMEM((1, count), F32),
            pltpu.VMEM((24 * count // CHUNK, CHUNK), F32),
            pltpu.VMEM((groups, count), BF16),
            pltpu.VMEM((3 * FIELDS * LANES // owned, count), BF16),
            pltpu.SemaphoreType.DMA((6,)),
        ],
        compiler_params=params,
        name="send",
    )(
        me,
        *(
            pltpu.with_memory_space_constraint(x, pltpu.HBM)
            for x in (label_row, owner_row, cap_row, positions, velocities, masses.reshape(1, count))
        ),
    )
    received = exchange(outgoing, FIELDS)
    answers, catalog = pl.pallas_call(
        functools.partial(owner_kernel, devices, owned),
        out_shape=(
            jax.ShapeDtypeStruct((devices * 2, LANES), F32),
            jax.ShapeDtypeStruct((4, owned), F32),
        ),
        scratch_shapes=[pltpu.VMEM((2, devices * 8, LANES), F32)],
        compiler_params=params,
        name="owner",
    )(received, limit)
    returned = exchange(answers, 2)
    index, potential, binding = pl.pallas_call(
        functools.partial(final_kernel, devices, owned),
        out_shape=(
            jax.ShapeDtypeStruct((1, count), jnp.int32),
            jax.ShapeDtypeStruct((1, count), F32),
            jax.ShapeDtypeStruct((1, count), F32),
        ),
        compiler_params=params,
        name="final",
    )(rank, hit, order, velocities, returned)
    return index.reshape(count), potential.reshape(count), binding.reshape(count), catalog


def solution(mesh):
    return jax.shard_map(
        shards,
        mesh=mesh,
        in_specs=(
            P(None, ("gx", "gy")),
            P(None, ("gx", "gy")),
            P(("gx", "gy")),
            P(("gx", "gy"), None),
            P(),
            P(),
        ),
        out_specs=(P(("gx", "gy")), P(("gx", "gy")), P(("gx", "gy")), P(None, ("gx", "gy"))),
        check_vma=False,
    )
```

```python
import functools

import jax
import jax.numpy as jnp
from jax import lax
from jax.experimental import pallas as pl
from jax.experimental.pallas import tpu as pltpu
from jax.sharding import PartitionSpec as P

CAP = 2048
LANES = 128
CHUNK = 256
FIELDS = 7
softening_sq = 0.0025
F32 = jnp.float32
BF16 = jnp.bfloat16


def iota(shape, axis):
    return lax.broadcasted_iota(jnp.int32, shape, axis)


def parts_of(x):
    high = x.astype(BF16).astype(F32)
    rest = x - high
    middle = rest.astype(BF16).astype(F32)
    return high, middle, rest - middle


def inverse_column(owner_row, slots):
    groups = owner_row.shape[1]
    ids = iota((groups, groups), 1).astype(F32)
    return jnp.sum(jnp.where(owner_row == slots, ids, 0.0), axis=1, keepdims=True)


def send_kernel(
    devices, owned, me_ref, label_hbm, owner_hbm, cap_hbm, pos_hbm, vel_hbm, mass_hbm,
    out_ref, rank_ref, limit_ref, hit_out, order_ref,
    label_ref, owner_ref, cap_ref, pos_ref, vel_ref, mass_ref, parts_ref, hit_ref, spread_ref, sems,
):
    count = label_ref.shape[1]
    groups = devices * owned
    span = LANES // owned
    chunks = count // CHUNK
    copies = [
        pltpu.make_async_copy(source, target, sems.at[k])
        for k, (source, target) in enumerate(
            (
                (owner_hbm, owner_ref),
                (label_hbm, label_ref),
                (pos_hbm, pos_ref),
                (vel_hbm, vel_ref),
                (mass_hbm, mass_ref),
                (cap_hbm, cap_ref),
            )
        )
    ]
    for copy in copies:
        copy.start()
    rows = iota((groups, 1), 0)
    upto = (iota((CHUNK, CHUNK), 0) <= iota((CHUNK, CHUNK), 1)).astype(F32).astype(BF16)
    copies[0].wait()
    inverse = inverse_column(owner_ref[...], (rows % devices) * owned + rows // devices)
    for copy in copies[1:]:
        copy.wait()

    kind = BF16 if groups <= 256 else F32
    name = jnp.broadcast_to(inverse, (groups, CHUNK)).astype(kind)
    for chunk in range(chunks):
        cols = slice(chunk * CHUNK, (chunk + 1) * CHUNK)
        label = jnp.broadcast_to(label_ref[:, cols].astype(F32), (16, CHUNK)).astype(kind)
        for row in range(0, groups, 16):
            here = slice(row, row + 16)
            hit = jnp.where(label == name[here], jnp.ones((), kind), jnp.zeros((), kind)).astype(BF16)
            hit_ref[here, cols] = hit
            hit_out[here, cols] = hit
    prefixes = [jnp.dot(hit_ref[:, chunk * CHUNK : (chunk + 1) * CHUNK], upto, preferred_element_type=F32) for chunk in range(chunks)]

    fields = jnp.concatenate([pos_ref[...], vel_ref[...], mass_ref[...], jnp.zeros((1, count), F32)], axis=0)
    for k, part in enumerate(parts_of(fields)):
        for chunk in range(chunks):
            parts_ref[chunk * 24 + k * 8 : chunk * 24 + k * 8 + 8, :] = part[:, chunk * CHUNK : (chunk + 1) * CHUNK]

    base = jnp.zeros((groups, CHUNK), BF16)
    ranks = iota((span, 1), 0).astype(F32)
    for chunk in range(chunks):
        cols = slice(chunk * CHUNK, (chunk + 1) * CHUNK)
        prefix = prefixes[chunk]
        mine = (prefix.astype(BF16) + base) * hit_ref[:, cols]
        base = base + jnp.broadcast_to(prefix[:, CHUNK - 1 : CHUNK], (groups, CHUNK)).astype(BF16)
        while mine.shape[0] > 16:
            half = mine.shape[0] // 2
            mine = mine[0:half] + mine[half:]
        rank = jnp.sum(mine.astype(F32), axis=0, keepdims=True) - 1.0
        for part in range(CHUNK // LANES):
            line = chunk * (CHUNK // LANES) + part
            rank_ref[line : line + 1, :] = rank[:, part * LANES : (part + 1) * LANES]
        here = rank == ranks
        for k in range(3):
            for f in range(FIELDS):
                row = parts_ref[pl.ds(chunk * 24 + k * 8 + f, span, stride=0), :]
                first = (k * FIELDS + f) * span
                spread_ref[first : first + span, cols] = jnp.where(
                    here, row, 0.0
                ).astype(BF16)

    found = lax.dot_general(
        spread_ref[...], hit_ref[...], (((1,), (1,)), ((), ())), preferred_element_type=F32
    )
    size = FIELDS * span
    found = (found[0:size] + found[size : 2 * size]) + found[2 * size :]
    slots = me_ref[0, 0] * owned + iota((owned, 1), 0)
    limit_col = jnp.sum(
        jnp.where(owner_ref[...] == slots, jnp.minimum(cap_ref[...], CAP).astype(F32), 0.0),
        axis=1,
        keepdims=True,
    )
    segment = iota((1, LANES), 1) // span
    limit_ref[...] = jnp.sum(
        jnp.where(segment == iota((owned, 1), 0), limit_col, 0.0), axis=0, keepdims=True
    )
    inverse_row = jnp.sum(jnp.where(rows == iota((1, groups), 1), inverse, 0.0), axis=0, keepdims=True)
    order_ref[...] = jnp.where(inverse < inverse_row, 1.0, 0.0).astype(BF16)

    block = max(1, LANES // devices)
    upper = iota((1, LANES), 1) // devices
    tiles = []
    for tile in range(owned // block):
        lanes = slice(tile * LANES, (tile + 1) * LANES)
        piece = [found[f * span : (f + 1) * span, lanes] for f in range(FIELDS)]
        piece += [jnp.zeros((span, LANES), F32)] * (-FIELDS % block)
        step = block // 2
        while step:
            far = (upper & step) != 0
            for low in range(len(piece)):
                if low & step:
                    continue
                one, two = piece[low], piece[low + step]
                piece[low] = jnp.where(far, pltpu.roll(two, step * devices, 1), one)
                piece[low + step] = jnp.where(far, two, pltpu.roll(one, LANES - step * devices, 1))
            step //= 2
        tiles.append(piece)
    for first in range(0, FIELDS, block):
        turned = jnp.transpose(
            jnp.concatenate([piece[first + k] for piece in tiles for k in range(block)], axis=0)
        )
        for f in range(first, min(first + block, FIELDS)):
            low = (f - first) * devices
            out_ref[pl.ds(f, devices, stride=FIELDS), :] = turned[low : low + devices]


def owner_kernel(devices, owned, got_ref, limit_ref, out_ref, stats_ref, far_ref):
    span = LANES // owned
    blocks = devices // 8
    lane = iota((1, LANES), 1)
    offset = lane % span
    segment = lane // span

    def spin(x):
        return jnp.where(offset >= 1, pltpu.roll(x, 1, 1), pltpu.roll(x, LANES + 1 - span, 1))

    field = [got_ref[pl.ds(f, devices, stride=FIELDS), :] for f in range(FIELDS)]
    mass = field[6]
    valid = mass > 0.0

    limit = limit_ref[...]

    joined = (iota((LANES, 1), 0) // span == segment).astype(F32).astype(BF16)
    counts = jnp.dot(jnp.where(valid, 1.0, 0.0).astype(BF16), joined, preferred_element_type=F32)
    before = (iota((devices, devices), 1) < iota((devices, devices), 0)).astype(F32).astype(BF16)
    prefix = jnp.dot(before, counts.astype(BF16), preferred_element_type=F32)
    kept = jnp.minimum(jnp.sum(counts, axis=0, keepdims=True), limit)
    keep = valid & (prefix + offset.astype(F32) < limit)
    mass = jnp.where(keep, mass, 0.0)

    sums = jnp.concatenate(
        [jnp.sum(x, axis=0, keepdims=True) for x in (mass, mass * field[3], mass * field[4], mass * field[5])]
        + [jnp.zeros((4, LANES), F32)],
        axis=0,
    )
    turned = sums
    for _ in range(span - 1):
        turned = spin(turned)
        sums = sums + turned
    mass_sum = sums[0:1]
    bulk = sums[1:4] / mass_sum
    stats = jnp.concatenate([mass_sum / CAP, bulk, jnp.zeros((4, LANES), F32)], axis=0)
    columns = iota((1, owned), 1)
    table = jnp.zeros((8, owned), F32)
    for group in range(owned):
        table = jnp.where(columns == group, stats[:, group * span : group * span + 1], table)
    stats_ref[...] = table[0:4]

    near = [[x[b * 8 : b * 8 + 8] for b in range(blocks)] for x in (field[0], field[1], field[2], mass)]

    def pair_block(turned, diagonal, one_way, slot, acc):
        acc = list(acc)
        far_sum = [None] * blocks
        for k in range(4 * blocks):
            far_ref[slot, k * 16 : k * 16 + 8, :] = turned[k]
            far_ref[slot, k * 16 + 8 : k * 16 + 16, :] = turned[k]
        for shift in range(8):
            on_diag = shift in diagonal
            single = shift in one_way
            for b in range(blocks):
                others = list(range(b))
                if on_diag or single:
                    others.append(b)
                if not others:
                    continue
                far = [turned[k * blocks + b] for k in range(4)]
                if shift:
                    starts = [(k * blocks + b) * 16 + shift for k in range(4)]
                    far = [far_ref[slot, start : start + 8, :] for start in starts]
                back = None
                for a in others:
                    dx = near[0][a] - far[0]
                    dy = near[1][a] - far[1]
                    dz = near[2][a] - far[2]
                    inverse = lax.rsqrt((dx * dx + dy * dy) + (dz * dz + softening_sq))
                    acc[a] = acc[a] + far[3] * inverse
                    if a == b and single:
                        continue
                    term = near[3][a] * inverse
                    back = term if back is None else back + term
                if back is not None:
                    if shift:
                        back = pltpu.roll(back, shift, 0)
                    far_sum[b] = back if far_sum[b] is None else far_sum[b] + back
        far_sum = [jnp.zeros((8, LANES), F32) if x is None else x for x in far_sum]
        return acc, far_sum

    half = span // 2
    every = tuple(range(8))
    flat = [near[k][b] for k in range(4) for b in range(blocks)]
    zeros = [jnp.zeros((8, LANES), F32)] * blocks

    def turn(diagonal, one_way, step, carry):
        turned, acc, far = carry
        turned = [spin(x) for x in turned]
        acc, extra = pair_block(turned, diagonal, one_way, step % 2, acc)
        far = [spin(x + y) for x, y in zip(far, extra)]
        return turned, acc, far

    def repeat(diagonal, carry):
        if blocks > 4:
            return lax.fori_loop(1, half, functools.partial(turn, diagonal, ()), carry)
        for step in range(1, half):
            carry = turn(diagonal, (), step, carry)
        return carry

    carry = repeat((), (flat, zeros, zeros))
    carry = turn((1, 2, 3), (0, 4), 0, carry)
    carry = repeat(every, carry)
    _, acc, far = carry
    acc, extra = pair_block(flat, (1, 2, 3), (4,), 0, acc)
    pot = jnp.concatenate([x + (y + z) for x, y, z in zip(acc, far, extra)], axis=0) / -CAP

    wide = functools.partial(jnp.broadcast_to, shape=(devices, LANES))
    more = jnp.where(offset == 3, prefix, wide(kept))
    for axis in range(3):
        more = jnp.where(offset == axis, wide(bulk[axis : axis + 1]), more)
    out_ref[pl.ds(0, devices, stride=2), :] = pot
    out_ref[pl.ds(1, devices, stride=2), :] = more


def final_kernel(devices, owned, rank_ref, hit_ref, order_ref, vel_ref, got_ref, index_ref, pot_ref, bind_ref, dense_ref):
    count = vel_ref.shape[1]
    groups = devices * owned
    span = LANES // owned
    used = 2 * span
    block = max(1, LANES // devices)
    both = [got_ref[pl.ds(k, devices, stride=2), :] for k in range(2)]
    both += [jnp.zeros((-2 * devices % LANES, LANES), F32)] if 2 * devices % LANES else []
    turned = jnp.transpose(jnp.concatenate(both, axis=0))
    place = iota((1, LANES), 1) // devices
    table = []
    for k in range(2):
        tile, offset = divmod(k * devices, LANES)
        row = []
        for first in range(0, owned, block):
            filled = None
            for j in range(block):
                piece = turned[(first + j) * span : (first + j + 1) * span, tile * LANES : (tile + 1) * LANES]
                shift = (j * devices - offset) % LANES
                piece = pltpu.roll(piece, shift, 1) if shift else piece
                filled = piece if filled is None else jnp.where(place == j, piece, filled)
            row.append(filled)
        table.append(jnp.concatenate(row, axis=1))
    table = jnp.concatenate(table, axis=0)
    parts = parts_of(table)
    counted = jnp.concatenate([part[used - 8 :] for part in parts[0:2]], axis=0).astype(BF16)
    starts = jnp.dot(counted, order_ref[...], preferred_element_type=F32)
    starts = jnp.broadcast_to(starts[7:8] + starts[15:16], (8, groups))
    parts = jnp.concatenate([*parts, *parts_of(starts)], axis=0).astype(BF16)
    lines = CHUNK // LANES
    for chunk in range(count // CHUNK):
        cols = slice(chunk * CHUNK, (chunk + 1) * CHUNK)
        rank = jnp.concatenate(
            [rank_ref[line : line + 1, :] for line in range(chunk * lines, (chunk + 1) * lines)], axis=1
        )
        found = jnp.dot(parts, hit_ref[:, cols], preferred_element_type=F32)
        start = (found[3 * used : 3 * used + 1] + found[3 * used + 8 : 3 * used + 9]) + found[
            3 * used + 16 : 3 * used + 17
        ]
        found = (found[0:used] + found[used : 2 * used]) + found[2 * used : 3 * used]
        pot = jnp.sum(
            jnp.where(iota((span, 1), 0).astype(F32) == rank, found[0:span], 0.0), axis=0, keepdims=True
        )
        speed = jnp.sum((vel_ref[:, cols] - found[span : span + 3]) ** 2, axis=0, keepdims=True)
        values = (pot, speed, found[span + 3 : span + 4], found[used - 1 : used], start)
        for k, value in enumerate(values):
            for part in range(lines):
                line = chunk * lines + part
                dense_ref[k, line : line + 1, :] = value[:, part * LANES : (part + 1) * LANES]
    pot, speed, prefix, kept, start = [dense_ref[k] for k in range(5)]
    global_rank = prefix + rank_ref[...]
    keep = global_rank < kept
    index_ref[...] = jnp.where(keep, (start + global_rank).astype(jnp.int32), -1)
    pot_ref[...] = jnp.where(keep, pot, 0.0)
    bind_ref[...] = jnp.where(keep, 0.5 * speed + pot, 0.0)


def shards(positions, velocities, masses, labels, owner_slot, group_cap):
    count = labels.shape[0]
    groups = owner_slot.shape[0]
    devices = lax.axis_size(("gx", "gy"))
    owned = groups // devices
    label_row = labels.reshape(1, count)
    owner_row = owner_slot.reshape(1, groups)
    cap_row = group_cap.reshape(1, groups)
    me = lax.axis_index(("gx", "gy")).astype(jnp.int32).reshape(1, 1)
    params = pltpu.CompilerParams(vmem_limit_bytes=min(48, 8 * groups // 128) * 1024 * 1024)

    def exchange(x, rows):
        flat = x.reshape(devices * rows * LANES)
        flat = lax.all_to_all(flat, ("gx", "gy"), split_axis=0, concat_axis=0, tiled=True)
        return flat.reshape(devices * rows, LANES)

    outgoing, rank, limit, hit, order = pl.pallas_call(
        functools.partial(send_kernel, devices, owned),
        out_shape=(
            jax.ShapeDtypeStruct((devices * FIELDS, LANES), F32),
            jax.ShapeDtypeStruct((count // LANES, LANES), F32),
            jax.ShapeDtypeStruct((1, LANES), F32),
            jax.ShapeDtypeStruct((groups, count), BF16),
            jax.ShapeDtypeStruct((groups, groups), BF16),
        ),
        in_specs=[pl.BlockSpec(memory_space=pltpu.SMEM)] + [pl.BlockSpec(memory_space=pltpu.HBM)] * 6,
        scratch_shapes=[
            pltpu.VMEM((1, count), jnp.int32),
            pltpu.VMEM((1, groups), jnp.int32),
            pltpu.VMEM((1, groups), jnp.int32),
            pltpu.VMEM((3, count), F32),
            pltpu.VMEM((3, count), F32),
            pltpu.VMEM((1, count), F32),
            pltpu.VMEM((24 * count // CHUNK, CHUNK), F32),
            pltpu.VMEM((groups, count), BF16),
            pltpu.VMEM((3 * FIELDS * LANES // owned, count), BF16),
            pltpu.SemaphoreType.DMA((6,)),
        ],
        compiler_params=params,
        name="send",
    )(
        me,
        *(
            pltpu.with_memory_space_constraint(x, pltpu.HBM)
            for x in (label_row, owner_row, cap_row, positions, velocities, masses.reshape(1, count))
        ),
    )
    received = exchange(outgoing, FIELDS)
    answers, catalog = pl.pallas_call(
        functools.partial(owner_kernel, devices, owned),
        out_shape=(
            jax.ShapeDtypeStruct((devices * 2, LANES), F32),
            jax.ShapeDtypeStruct((4, owned), F32),
        ),
        scratch_shapes=[pltpu.VMEM((2, devices * 8, LANES), F32)],
        compiler_params=params,
        name="owner",
    )(received, limit)
    returned = exchange(answers, 2)
    index, potential, binding = pl.pallas_call(
        functools.partial(final_kernel, devices, owned),
        out_shape=(
            jax.ShapeDtypeStruct((count // LANES, LANES), jnp.int32),
            jax.ShapeDtypeStruct((count // LANES, LANES), F32),
            jax.ShapeDtypeStruct((count // LANES, LANES), F32),
        ),
        scratch_shapes=[pltpu.VMEM((5, count // LANES, LANES), F32)],
        compiler_params=params,
        name="final",
    )(rank, hit, order, velocities, returned)
    return index.reshape(count), potential.reshape(count), binding.reshape(count), catalog


def solution(mesh):
    return jax.shard_map(
        shards,
        mesh=mesh,
        in_specs=(
            P(None, ("gx", "gy")),
            P(None, ("gx", "gy")),
            P(("gx", "gy")),
            P(("gx", "gy"), None),
            P(),
            P(),
        ),
        out_specs=(P(("gx", "gy")), P(("gx", "gy")), P(("gx", "gy")), P(None, ("gx", "gy"))),
        check_vma=False,
    )
```
